32 devices in a mesh: gx: 4 (over y, core), gy: 8 (over z, x).
Axes of the slice: x: 2, y: 2, z: 4, core: 2. Of those that a mesh axis runs over, the one named last changes fastest.
Arguments:
- a_rows: bfloat16 [196608, 1024], P(('gx', 'gy')), may hold values from -6 to 6
- heights: int32 [32], P('gx'), may hold values from 1 to 38, as said below
- destination: int32 [32, 48], P('gx'), may hold values from 0 to 1023, as said below
Outputs:
- ortho_rows: bfloat16 [131072, 1024], P(('gx', 'gy'))
- factor_r: float32 [1024, 1024], replicated
The draws below stay inside these ranges and needn't reach their ends.
Inputs may be any that keep to these rules, and one draw needn't show every extreme that they name: Tiles 0 to heights[d] - 1 of device d are live, the others carry nothing of the problem; the largest value is reached in every draw. For a live tile, destination // 32 is a device with the same gx index as the tile's device; live tiles name distinct slots; one device sends at most one live tile to any other device; entries of tiles that are not live are meaningless.
All inputs are finite; a program needn't handle non-finite values.
Results may differ from the reference program's by a relative error of at most 0.00055.
Values may be sent and summed in bfloat16 or wider, within the bound.
A program may use at most 256 MiB of HBM per device.

```python
import math
import jax
import jax.numpy as jnp
from jax import lax

W = 1024
TILE = 128
SLOTS = 32
TILES = 48
N_GY = 8
DEVICES = 32


def plan_tiles(key):
    base = jax.random.fold_in(key, 7)
    keys = jax.random.split(base, 6)
    group_size = N_GY
    groups = DEVICES // group_size
    heavy_count = group_size // 4
    light_count = group_size - heavy_count
    extra = min(TILES - SLOTS, light_count)
    ordering = jax.vmap(lambda sub: jax.random.permutation(sub, group_size))(jax.random.split(keys[0], groups)).astype(jnp.int32)
    ranking = jnp.argsort(ordering, axis=1).astype(jnp.int32)
    heavy = ranking < heavy_count
    high = jax.random.randint(keys[1], (groups, group_size), SLOTS + 1, SLOTS + extra + 1)
    high = jnp.where(ranking == 0, SLOTS + extra, high)
    small = jax.random.randint(keys[2], (groups, group_size), 1, SLOTS - heavy_count + 1)
    height = jnp.where(heavy, high, small).astype(jnp.int32)
    excess_rank = jnp.take_along_axis(height, ordering, 1) - SLOTS
    flat_height = height.reshape(-1)
    tile_perm = jax.vmap(lambda sub: jax.random.permutation(sub, TILES))(jax.random.split(keys[3], DEVICES)).astype(jnp.int32)
    tile_ids = jnp.arange(TILES, dtype=jnp.int32)
    tile_live = tile_ids[None, :] < flat_height[:, None]
    tile_order = jnp.argsort(jnp.where(tile_live, tile_perm, tile_perm + TILES), axis=1).astype(jnp.int32)
    position = jnp.argsort(tile_order, axis=1).astype(jnp.int32)
    kept = jnp.minimum(flat_height, SLOTS)
    rank_flat = ranking.reshape(-1)
    offset = position - kept[:, None]
    leaving = tile_live & (offset >= 0)
    light_target = jnp.mod(rank_flat[:, None] + offset, light_count)
    group_ids = jnp.arange(DEVICES, dtype=jnp.int32) // group_size
    target_gy = jnp.take_along_axis(ordering[group_ids], heavy_count + light_target, 1)
    device_ids = jnp.arange(DEVICES, dtype=jnp.int32)
    target_dev = jnp.where(leaving, group_ids[:, None] * group_size + target_gy, device_ids[:, None])
    heavy_ids = jnp.arange(heavy_count, dtype=jnp.int32)
    light_ids = jnp.arange(light_count, dtype=jnp.int32)
    sends = jnp.mod(light_ids[None, :] - heavy_ids[:, None], light_count)[None] < excess_rank[:, :heavy_count, None]
    sends_int = sends.astype(jnp.int32)
    before = jnp.cumsum(sends_int, axis=1) - sends_int
    slot_perm = jax.vmap(lambda sub: jax.random.permutation(sub, SLOTS))(jax.random.split(keys[4], DEVICES)).astype(jnp.int32)
    kept_slot = jnp.take_along_axis(slot_perm, jnp.minimum(position, SLOTS - 1), 1)
    sender_rank = jnp.broadcast_to(jnp.minimum(rank_flat, heavy_count - 1)[:, None], (DEVICES, TILES))
    group_grid = jnp.broadcast_to(group_ids[:, None], (DEVICES, TILES))
    recv_rank = before[group_grid, sender_rank, light_target]
    recv_kept = kept[target_dev]
    sent_slot = slot_perm[target_dev, jnp.minimum(recv_kept + recv_rank, SLOTS - 1)]
    chosen_slot = jnp.where(leaving, sent_slot, kept_slot)
    filler = jax.random.randint(keys[5], (DEVICES, TILES), 0, DEVICES * SLOTS)
    mapped = jnp.where(tile_live, target_dev * SLOTS + chosen_slot, filler)
    return (flat_height.astype(jnp.int32), mapped.astype(jnp.int32))


def draw_heights(key, part):
    return plan_tiles(key)[0]


def draw_destination(key, part):
    return plan_tiles(key)[1]


def raised(array, stream_key, source, target, blocks, factor):
    def block_of(dim):
        return (jnp.arange(array.shape[dim]) // (array.shape[dim] // blocks)).reshape((-1,) + (1,) * (array.ndim - 1 - dim))

    near = jax.random.permutation(stream_key, blocks)[block_of(target)]
    far = (block_of(target) + blocks // 2) % blocks
    return jnp.where((block_of(source) == near) | (block_of(source) == far), factor * array, array)


def shard_levels(own_key, extent, cuts, smallest, top_value):
    def one(dim, parts):
        steps = jax.random.uniform(jax.random.fold_in(jax.random.fold_in(own_key, 6), dim), (parts,), jnp.float32, smallest / len(cuts), top_value / len(cuts))
        return jnp.repeat(jnp.exp(steps), extent[dim] // parts).reshape((-1,) + (1,) * (len(extent) - dim - 1))

    gain = one(*cuts[0])
    for cut in cuts[1:]:
        gain = gain * one(*cut)
    return gain


def bell_draw_with(stream_key, dims, scale, reach, shards, heavy, kind=jnp.bfloat16):
    result = scale * jax.random.normal(stream_key, dims, jnp.float32)
    if shards:
        result = result * shard_levels(stream_key, dims, shards, -0.22, 0.18)
    return jnp.clip(raised(result, jax.random.fold_in(stream_key, 3), *heavy), -reach, reach).astype(kind)


def setup_inputs(seed: int = 0) -> dict:
    seeds = jax.random.split(jax.random.key(seed), 4)
    a_rows = bell_draw_with(seeds[0], (DEVICES * TILES * TILE, W), 1.0, 6.0, ((0, 32),), (0, 1, 32, 2.75))
    heights = draw_heights(jax.random.fold_in(seeds[3], 71), 0)
    destination = draw_destination(jax.random.fold_in(seeds[3], 71), 0)
    return dict(a_rows=a_rows, heights=heights, destination=destination)


def reference(a_rows, heights, destination):
    dev_count = heights.shape[0]
    tile_stack = a_rows.reshape(dev_count * TILES, TILE, W)
    tile_live = (jnp.arange(TILES, dtype=jnp.int32)[None, :] < heights[:, None]).reshape(-1)
    target = jnp.where(tile_live, destination.reshape(-1), dev_count * SLOTS).astype(jnp.int32)
    balanced = jnp.zeros((dev_count * SLOTS, TILE, W), jnp.bfloat16).at[target].set(tile_stack, mode='drop')
    slabs = balanced.reshape(dev_count, SLOTS * TILE, W)

    def accumulate(running, slab_rows):
        product = lax.dot_general(slab_rows.astype(jnp.float32), slab_rows.astype(jnp.float32), (((0,), (0,)), ((), ())), preferred_element_type=jnp.float32)
        return (running + product, None)
    gram, _ = lax.scan(accumulate, jnp.zeros((W, W), jnp.float32), slabs)
    low_factor = jnp.linalg.cholesky(gram)
    root_scale = math.sqrt(dev_count * SLOTS * TILE)

    def orthonormal(slab_rows):
        solved = jax.scipy.linalg.solve_triangular(low_factor, slab_rows.astype(jnp.float32).T, lower=True)
        return (solved.T * root_scale).astype(jnp.bfloat16)
    ortho_rows = lax.map(orthonormal, slabs).reshape(-1, W)
    return (ortho_rows, low_factor.T / root_scale)
```

```python
import functools
import math

import jax
import jax.numpy as jnp
from jax import lax
from jax.experimental import pallas as pl
from jax.experimental.pallas import tpu as pltpu
from jax.sharding import PartitionSpec as P

TILE = 128
SLOTS = 32
GROUP = 4
BIG = 256
PANEL = 4
NT = (((1,), (1,)), ((), ()))
TN = (((0,), (0,)), ((), ()))
HIGHEST = lax.Precision.HIGHEST


def gram_kernel(height_ref, a_ref, out_ref):
    step = pl.program_id(0)
    rows, breadth = a_ref.shape
    live = height_ref[0] * TILE - step * rows

    @pl.when(step == 0)
    def _():
        out_ref[...] = jnp.zeros_like(out_ref)

    def add(block):
        across = block.T
        place = 0
        for i in range(breadth // BIG):
            width = (i + 1) * BIG
            product = lax.dot_general(
                across[i * BIG : (i + 1) * BIG],
                block[:, :width],
                (((1,), (0,)), ((), ())),
                preferred_element_type=jnp.float32,
            )
            for j in range(i + 1):
                out_ref[place] += product[:, j * BIG : (j + 1) * BIG]
                place += 1

    @pl.when(live >= rows)
    def _():
        add(a_ref[...])

    @pl.when((live > 0) & (live < rows))
    def _():
        index = lax.broadcasted_iota(jnp.int32, (rows, breadth), 0)
        keep = (index < live).astype(jnp.float32).astype(a_ref.dtype)
        add(a_ref[...] * keep)


def local_gram(a_rows, height):
    total, breadth = a_rows.shape
    rows = GROUP * TILE
    blocks = breadth // BIG
    packed = blocks * (blocks + 1) // 2
    return pl.pallas_call(
        gram_kernel,
        out_shape=jax.ShapeDtypeStruct((packed, BIG, BIG), jnp.float32),
        grid_spec=pltpu.PrefetchScalarGridSpec(
            num_scalar_prefetch=1,
            grid=(total // rows,),
            in_specs=[
                pl.BlockSpec(
                    (rows, breadth),
                    lambda i, h: (jnp.minimum(i, (h[0] - 1) // GROUP), 0),
                )
            ],
            out_specs=pl.BlockSpec((packed, BIG, BIG), lambda i, h: (0, 0, 0)),
        ),
        cost_estimate=pl.CostEstimate(
            flops=total * breadth * breadth, bytes_accessed=total * breadth * 2, transcendentals=0
        ),
        name="gram",
    )(height, a_rows)


def eliminate(block):
    lane = lax.broadcasted_iota(jnp.int32, (1, TILE), 1)
    sub = lax.broadcasted_iota(jnp.int32, (8, TILE), 0)
    parts = [block[8 * g : 8 * g + 8] for g in range(TILE // 8)]
    for first in range(0, TILE, PANEL):
        start = first // 8
        spread = [
            [jnp.broadcast_to(part[:, first + m : first + m + 1], (8, TILE)) for part in parts[start:]]
            for m in range(PANEL)
        ]
        for m in range(PANEL):
            at = first + m
            local = at % 8
            column = spread[m]
            pivot = jnp.broadcast_to(column[0][local : local + 1], (8, TILE))
            inverse = 1.0 / pivot
            factors = [c * inverse for c in column]
            below = sub > local
            factors[0] = jnp.where(below, factors[0], 0.0)
            here = lane == at
            row = jnp.where(here, 1.0, parts[start][local : local + 1])
            row = jnp.broadcast_to(row, (8, TILE))
            for g in range(start, len(parts)):
                clear = here & below if g == start else here
                parts[g] = jnp.where(clear, 0.0, parts[g]) - factors[g - start] * row
            for n in range(m + 1, PANEL):
                level = jnp.broadcast_to(spread[n][0][local : local + 1], (8, TILE))
                spread[n] = [c - f * level for c, f in zip(spread[n], factors)]
    return jnp.concatenate(parts, axis=0)


def factor_kernel(root_scale, gram_ref, r_ref, high_ref, low_ref, work, line):
    breadth = r_ref.shape[0]
    count = breadth // TILE
    place = 0
    for i in range(breadth // BIG):
        for j in range(i + 1):
            block = gram_ref[place]
            work[i * BIG : (i + 1) * BIG, j * BIG : (j + 1) * BIG] = block
            if j < i:
                work[j * BIG : (j + 1) * BIG, i * BIG : (i + 1) * BIG] = block.T
            place += 1
    rows_id = lax.broadcasted_iota(jnp.int32, (TILE, TILE), 0)
    cols_id = lax.broadcasted_iota(jnp.int32, (TILE, TILE), 1)
    wide_id = lax.broadcasted_iota(jnp.int32, (TILE, breadth), 1)

    def step(k, carry):
        base = pl.multiple_of(k * TILE, TILE)
        mine = pl.ds(base, TILE)
        done = eliminate(work[mine, mine])
        diagonal = jnp.sum(jnp.where(rows_id == cols_id, done, 0.0), axis=1, keepdims=True)
        shrink = 1.0 / jnp.sqrt(diagonal)
        inverse = jnp.where(
            rows_id > cols_id, done, jnp.where(rows_id == cols_id, 1.0, 0.0)
        ) * shrink
        upper = jnp.where(rows_id <= cols_id, done, 0.0) * shrink
        line[...] = jnp.dot(
            inverse, work[mine, :], precision=HIGHEST, preferred_element_type=jnp.float32
        )
        r_ref[mine, :] = jnp.where(wide_id >= base, line[...], 0.0) * (1.0 / root_scale)
        r_ref[mine, mine] = upper * (1.0 / root_scale)
        line[:, mine] = inverse
        solved = jnp.where(wide_id < base + TILE, line[...], 0.0)
        high = solved.astype(jnp.bfloat16)
        high_ref[mine, :] = high
        low_ref[mine, :] = (solved - high.astype(jnp.float32)).astype(jnp.bfloat16)

        def update(i, carry):
            theirs = pl.ds(pl.multiple_of(i * TILE, TILE), TILE)
            left = lax.dot_general(
                work[theirs, mine], inverse, NT, precision=HIGHEST, preferred_element_type=jnp.float32
            )
            work[theirs, mine] = jnp.zeros((TILE, TILE), jnp.float32)
            work[theirs, :] -= jnp.dot(
                left, line[...], precision=HIGHEST, preferred_element_type=jnp.float32
            )
            return carry

        lax.fori_loop(k + 1, count, update, 0)
        return carry

    lax.fori_loop(0, count, step, 0)


def factor(packed, breadth, root_scale):
    square = (breadth, breadth)
    return pl.pallas_call(
        functools.partial(factor_kernel, root_scale),
        out_shape=(
            jax.ShapeDtypeStruct(square, jnp.float32),
            jax.ShapeDtypeStruct(square, jnp.bfloat16),
            jax.ShapeDtypeStruct(square, jnp.bfloat16),
        ),
        in_specs=[pl.BlockSpec(memory_space=pltpu.VMEM)],
        out_specs=tuple(pl.BlockSpec(memory_space=pltpu.VMEM) for _ in range(3)),
        scratch_shapes=[
            pltpu.VMEM(square, jnp.float32),
            pltpu.VMEM((TILE, breadth), jnp.float32),
        ],
        name="factor",
    )(packed)


def ortho_kernel(root_scale, own_at, in_at, kind, *refs):
    own, come = refs[:GROUP], refs[GROUP : 2 * GROUP]
    high_ref, low_ref, out_ref, block = refs[2 * GROUP :]
    step = pl.program_id(0)
    breadth = out_ref.shape[1]
    for g in range(GROUP):
        which = kind[step * GROUP + g]
        rows = pl.ds(g * TILE, TILE)

        @pl.when(which == 0)
        def _():
            block[rows, :] = jnp.zeros((TILE, breadth), block.dtype)

        @pl.when(which == 1)
        def _():
            block[rows, :] = own[g][...]

        @pl.when(which == 2)
        def _():
            block[rows, :] = come[g][...]

    for j in range(breadth // BIG):
        cols = slice(j * BIG, (j + 1) * BIG)
        width = (j + 1) * BIG
        left = block[:, :width]
        product = lax.dot_general(
            left, high_ref[cols, :width], NT, preferred_element_type=jnp.float32
        ) + lax.dot_general(left, low_ref[cols, :width], NT, preferred_element_type=jnp.float32)
        out_ref[:, cols] = (product * root_scale).astype(out_ref.dtype)


def carried(index, used):
    index = index.reshape(-1, GROUP)
    used = used.reshape(-1, GROUP)
    steps = jnp.arange(index.shape[0], dtype=jnp.int32)
    earlier = used[None, :, :] & (steps[None, :, None] <= steps[:, None, None])
    last = jnp.max(jnp.where(earlier, steps[None, :, None], -1), axis=1)
    pick = last[:, None, :] == steps[None, :, None]
    return jnp.sum(jnp.where(pick, index[None], 0), axis=1).reshape(-1)


def orthonormal(a_rows, received, own_at, in_at, kind, high, low, root_scale):
    breadth = a_rows.shape[1]
    rows = GROUP * TILE

    def own_spec(g):
        return pl.BlockSpec((TILE, breadth), lambda s, o, c, k: (o[s * GROUP + g], 0))

    def in_spec(g):
        return pl.BlockSpec((TILE, breadth), lambda s, o, c, k: (c[s * GROUP + g], 0))

    whole = pl.BlockSpec((breadth, breadth), lambda s, o, c, k: (0, 0))
    return pl.pallas_call(
        functools.partial(ortho_kernel, root_scale),
        out_shape=jax.ShapeDtypeStruct((SLOTS * TILE, breadth), a_rows.dtype),
        grid_spec=pltpu.PrefetchScalarGridSpec(
            num_scalar_prefetch=3,
            grid=(SLOTS // GROUP,),
            in_specs=[own_spec(g) for g in range(GROUP)]
            + [in_spec(g) for g in range(GROUP)]
            + [whole, whole],
            out_specs=pl.BlockSpec((rows, breadth), lambda s, o, c, k: (s, 0)),
            scratch_shapes=[pltpu.VMEM((rows, breadth), a_rows.dtype)],
        ),
        name="ortho",
    )(own_at, in_at, kind, *([a_rows] * GROUP), *([received] * GROUP), high, low)


def on_device(a_rows, heights, destination):
    breadth = a_rows.shape[1]
    size_gy = lax.axis_size("gy")
    devices = lax.axis_size("gx") * size_gy
    group_pos = lax.axis_index("gy")
    my_index = lax.axis_index("gx") * size_gy + group_pos
    group_base = my_index - group_pos
    tile_stack = a_rows.reshape(-1, TILE, breadth)
    stored = tile_stack.shape[0]
    tile_ids = jnp.arange(stored, dtype=jnp.int32)
    peer_ids = jnp.arange(size_gy, dtype=jnp.int32)
    slot_ids = jnp.arange(SLOTS, dtype=jnp.int32)
    tile_live = tile_ids[None, :] < heights[:, None]
    target_dev = destination // SLOTS
    target_slot = destination % SLOTS
    own_live = tile_live[group_pos]
    own_dev = target_dev[group_pos]
    own_slot = target_slot[group_pos]
    leaving = own_live & (own_dev != my_index)
    chosen = leaving[None, :] & (own_dev[None, :] - group_base == peer_ids[:, None])
    send_index = jnp.sum(jnp.where(chosen, tile_ids[None, :], 0), axis=1)
    arriving = tile_live & (target_dev == my_index) & (peer_ids[:, None] != group_pos)
    arrive_slot = jnp.sum(jnp.where(arriving, target_slot, 0), axis=1)
    arrive_has = jnp.any(arriving, axis=1)
    staying = own_live & (own_dev == my_index)
    own_match = staying[None, :] & (own_slot[None, :] == slot_ids[:, None])
    in_match = arrive_has[None, :] & (arrive_slot[None, :] == slot_ids[:, None])
    own_has = jnp.any(own_match, axis=1)
    in_has = jnp.any(in_match, axis=1)
    own_at = carried(jnp.sum(jnp.where(own_match, tile_ids[None, :], 0), axis=1), own_has)
    in_at = carried(jnp.sum(jnp.where(in_match, peer_ids[None, :], 0), axis=1), in_has)
    kind = jnp.where(own_has, 1, jnp.where(in_has, 2, 0)).astype(jnp.int32)
    root_scale = math.sqrt(devices * SLOTS * TILE)
    received = lax.all_to_all(
        tile_stack[send_index], "gy", split_axis=0, concat_axis=0, tiled=True
    ).reshape(-1, breadth)
    packed = local_gram(a_rows, lax.dynamic_slice(heights, (group_pos,), (1,)))
    packed = lax.psum(packed, ("gx", "gy"))
    factor_r, high, low = factor(packed, breadth, root_scale)
    ortho_rows = orthonormal(a_rows, received, own_at, in_at, kind, high, low, root_scale)
    return (ortho_rows, factor_r)


def solution(mesh):
    placed = (P(("gx", "gy"), None), P("gx"), P("gx", None))
    return jax.shard_map(
        on_device,
        mesh=mesh,
        in_specs=placed,
        out_specs=(P(("gx", "gy"), None), P()),
        check_vma=False,
    )
```

```python
import functools
import math

import jax
import jax.numpy as jnp
from jax import lax
from jax.experimental import pallas as pl
from jax.experimental.pallas import tpu as pltpu
from jax.sharding import PartitionSpec as P

TILE = 128
SLOTS = 32
GROUP = 4
BIG = 256
PANEL = 8
REGS = TILE // 8
NT = (((1,), (1,)), ((), ()))
TN = (((0,), (0,)), ((), ()))
HIGHEST = lax.Precision.HIGHEST


def gram_kernel(height_ref, a_ref, out_ref):
    step = pl.program_id(0)
    rows, breadth = a_ref.shape
    live = height_ref[0] * TILE - step * rows

    @pl.when(step == 0)
    def _():
        out_ref[...] = jnp.zeros_like(out_ref)

    def add(block):
        across = block.T
        place = 0
        for i in range(breadth // BIG):
            width = (i + 1) * BIG
            product = lax.dot_general(
                across[i * BIG : (i + 1) * BIG],
                block[:, :width],
                (((1,), (0,)), ((), ())),
                preferred_element_type=jnp.float32,
            )
            for top in range(0, BIG, TILE):
                for j in range((i * BIG + top) // TILE + 1):
                    piece = product[top : top + TILE, j * TILE : (j + 1) * TILE]
                    out_ref[place : place + REGS] += piece.reshape(REGS, 8, TILE)
                    place += REGS

    @pl.when(live >= rows)
    def _():
        add(a_ref[...])

    @pl.when((live > 0) & (live < rows))
    def _():
        index = lax.broadcasted_iota(jnp.int32, (rows, breadth), 0)
        keep = (index < live).astype(jnp.float32).astype(a_ref.dtype)
        add(a_ref[...] * keep)


def local_gram(a_rows, height, split):
    total, breadth = a_rows.shape
    rows = GROUP * TILE
    blocks = breadth // TILE
    packed = pl.cdiv(blocks * (blocks + 1) // 2 * REGS, split) * split
    return pl.pallas_call(
        gram_kernel,
        out_shape=jax.ShapeDtypeStruct((packed, 8, TILE), jnp.float32),
        grid_spec=pltpu.PrefetchScalarGridSpec(
            num_scalar_prefetch=1,
            grid=(total // rows,),
            in_specs=[
                pl.BlockSpec(
                    (rows, breadth),
                    lambda i, h: (jnp.minimum(i, (h[0] - 1) // GROUP), 0),
                )
            ],
            out_specs=pl.BlockSpec((packed, 8, TILE), lambda i, h: (0, 0, 0)),
        ),
        cost_estimate=pl.CostEstimate(
            flops=total * breadth * breadth, bytes_accessed=total * breadth * 2, transcendentals=0
        ),
        name="gram",
    )(height, a_rows)


def eliminate(block):
    lane = lax.broadcasted_iota(jnp.int32, (1, TILE), 1)
    sub = lax.broadcasted_iota(jnp.int32, (8, TILE), 0)
    parts = [block[8 * g : 8 * g + 8] for g in range(TILE // 8)]
    for first in range(0, TILE, PANEL):
        start = first // 8
        spread = [
            [jnp.broadcast_to(part[:, first + m : first + m + 1], (8, TILE)) for part in parts[start:]]
            for m in range(PANEL)
        ]
        for m in range(PANEL):
            at = first + m
            local = at % 8
            column = spread[m]
            pivot = jnp.broadcast_to(column[0][local : local + 1], (8, TILE))
            inverse = 1.0 / pivot
            factors = [c * inverse for c in column]
            below = sub > local
            factors[0] = jnp.where(below, factors[0], 0.0)
            here = lane == at
            row = jnp.where(here, 1.0, parts[start][local : local + 1])
            row = jnp.broadcast_to(row, (8, TILE))
            for g in range(start, len(parts)):
                clear = here & below if g == start else here
                parts[g] = jnp.where(clear, 0.0, parts[g]) - factors[g - start] * row
            for n in range(m + 1, PANEL):
                level = jnp.broadcast_to(spread[n][0][local : local + 1], (8, TILE))
                spread[n] = [c - f * level for c, f in zip(spread[n], factors)]
    return jnp.concatenate(parts, axis=0)


def factor_kernel(root_scale, gram_ref, r_ref, high_ref, low_ref, work, line):
    breadth = r_ref.shape[0]
    count = breadth // TILE
    place = 0
    for i in range(count):
        for j in range(i + 1):
            block = gram_ref[place : place + REGS].reshape(TILE, TILE)
            work[i * TILE : (i + 1) * TILE, j * TILE : (j + 1) * TILE] = block
            if j < i:
                work[j * TILE : (j + 1) * TILE, i * TILE : (i + 1) * TILE] = block.T
            place += REGS
    rows_id = lax.broadcasted_iota(jnp.int32, (TILE, TILE), 0)
    cols_id = lax.broadcasted_iota(jnp.int32, (TILE, TILE), 1)
    wide_id = lax.broadcasted_iota(jnp.int32, (TILE, breadth), 1)

    def step(k, carry):
        base = pl.multiple_of(k * TILE, TILE)
        mine = pl.ds(base, TILE)
        done = eliminate(work[mine, mine])
        diagonal = jnp.sum(jnp.where(rows_id == cols_id, done, 0.0), axis=1, keepdims=True)
        shrink = 1.0 / jnp.sqrt(diagonal)
        inverse = jnp.where(
            rows_id > cols_id, done, jnp.where(rows_id == cols_id, 1.0, 0.0)
        ) * shrink
        upper = jnp.where(rows_id <= cols_id, done, 0.0) * shrink
        line[...] = jnp.dot(
            inverse, work[mine, :], precision=HIGHEST, preferred_element_type=jnp.float32
        )
        r_ref[mine, :] = jnp.where(wide_id >= base, line[...], 0.0) * (1.0 / root_scale)
        r_ref[mine, mine] = upper * (1.0 / root_scale)
        line[:, mine] = inverse
        solved = jnp.where(wide_id < base + TILE, line[...], 0.0)
        high = solved.astype(jnp.bfloat16)
        high_ref[mine, :] = high
        low_ref[mine, :] = (solved - high.astype(jnp.float32)).astype(jnp.bfloat16)

        def update(i, carry):
            theirs = pl.ds(pl.multiple_of(i * TILE, TILE), TILE)
            left = lax.dot_general(
                work[theirs, mine], inverse, NT, precision=HIGHEST, preferred_element_type=jnp.float32
            )
            work[theirs, mine] = jnp.zeros((TILE, TILE), jnp.float32)
            work[theirs, :] -= jnp.dot(
                left, line[...], precision=HIGHEST, preferred_element_type=jnp.float32
            )
            return carry

        lax.fori_loop(k + 1, count, update, 0)
        return carry

    lax.fori_loop(0, count, step, 0)


def reduce_kernel(sizes, x_ref, out_ref, work, *rest):
    streams = (("core", "x", "y", "z"), ("core", "y", "x", "z"))
    depth = len(streams[0])
    arrived, sends, recvs = rest[: 2 * depth], rest[2 * depth], rest[2 * depth + 1]
    at_gx, at_gy = lax.axis_index("gx"), lax.axis_index("gy")
    pair, across = sizes["core"], sizes["x"]
    here = {
        "core": lax.rem(at_gx, pair),
        "y": lax.div(at_gx, pair),
        "x": lax.rem(at_gy, across),
        "z": lax.div(at_gy, across),
    }

    def peer(dim, offset):
        there = dict(here)
        there[dim] = lax.rem(here[dim] + offset, sizes[dim])
        where = (there["y"] * pair + there["core"], there["z"] * across + there["x"])
        return there[dim], where

    barrier = pltpu.get_barrier_semaphore()
    greeted = 0
    for dim in streams[0]:
        for offset in range(1, sizes[dim]):
            pl.semaphore_signal(
                barrier, inc=1, device_id=peer(dim, offset)[1], device_id_type=pl.DeviceIdType.MESH
            )
            greeted += 1
    pl.semaphore_wait(barrier, greeted)

    half = x_ref.shape[0] // 2
    used = [0]

    def send(source, target, where):
        slot = used[0]
        used[0] += 1
        copy = pltpu.make_async_remote_copy(
            src_ref=source,
            dst_ref=target,
            send_sem=sends.at[slot],
            recv_sem=recvs.at[slot],
            device_id=where,
            device_id_type=pl.DeviceIdType.MESH,
        )
        copy.start()
        return copy

    pending = []
    base = [0, half]
    size = [half, half]
    bases = [[], []]

    def scatter(s, level):
        dim = streams[s][level]
        part = size[s] // sizes[dim]
        source = x_ref if level == 0 else work
        copies = []
        for offset in range(1, sizes[dim]):
            index, where = peer(dim, offset)
            copies.append(
                send(
                    source.at[pl.ds(base[s] + index * part, part)],
                    arrived[s * depth + level].at[offset - 1],
                    where,
                )
            )
        return copies

    def collect(s, level, copies):
        dim = streams[s][level]
        part = size[s] // sizes[dim]
        source = x_ref if level == 0 else work
        target = out_ref if level == depth - 1 else work
        mine = pl.ds(base[s] + here[dim] * part, part)
        for copy in copies:
            copy.wait_recv()
        total = source[mine]
        for offset in range(1, sizes[dim]):
            total += arrived[s * depth + level][offset - 1]
        target[mine] = total
        pending.extend(copies)
        base[s] = base[s] + here[dim] * part
        size[s] = part
        bases[s].append((base[s], part))

    def gather(s, level):
        start, part = bases[s][level]
        dim = streams[s][level]
        mine = out_ref.at[pl.ds(start, part)]
        return [send(mine, mine, peer(dim, offset)[1]) for offset in range(1, sizes[dim])]

    def landed(copies):
        for copy in copies:
            copy.wait_recv()
        pending.extend(copies)

    flying = [scatter(s, 0) for s in range(2)]
    for level in range(depth):
        for s in range(2):
            collect(s, level, flying[s])
            flying[s] = scatter(s, level + 1) if level + 1 < depth else gather(s, level)
    for level in reversed(range(depth)):
        for s in range(2):
            landed(flying[s])
            if level:
                flying[s] = gather(s, level - 1)
    for copy in pending:
        copy.wait_send()


def grid_sizes():
    size_gx, size_gy = lax.axis_size("gx"), lax.axis_size("gy")
    across = 1
    while across * across * 4 <= size_gy and size_gy % (across * 2) == 0:
        across *= 2
    pair = 2 if size_gx % 2 == 0 else 1
    return {"core": pair, "y": size_gx // pair, "x": across, "z": size_gy // across}


def reduce_all(packed, sizes):
    part = packed.shape[0] // 2
    buffers = []
    for order in (("core", "x", "y", "z"), ("core", "y", "x", "z")):
        left = part
        for dim in order:
            left //= sizes[dim]
            buffers.append(pltpu.VMEM((max(sizes[dim] - 1, 1), left, 8, TILE), jnp.float32))
    copies = 4 * sum(n - 1 for n in sizes.values())
    return pl.pallas_call(
        functools.partial(reduce_kernel, sizes),
        out_shape=jax.ShapeDtypeStruct(packed.shape, jnp.float32),
        in_specs=[pl.BlockSpec(memory_space=pltpu.VMEM)],
        out_specs=pl.BlockSpec(memory_space=pltpu.VMEM),
        scratch_shapes=[pltpu.VMEM(packed.shape, jnp.float32)]
        + buffers
        + [pltpu.SemaphoreType.DMA((copies,)), pltpu.SemaphoreType.DMA((copies,))],
        compiler_params=pltpu.CompilerParams(collective_id=0, has_side_effects=True),
        name="reduce_all",
    )(packed)


def factor(packed, breadth, root_scale):
    square = (breadth, breadth)
    return pl.pallas_call(
        functools.partial(factor_kernel, root_scale),
        out_shape=(
            jax.ShapeDtypeStruct(square, jnp.float32),
            jax.ShapeDtypeStruct(square, jnp.bfloat16),
            jax.ShapeDtypeStruct(square, jnp.bfloat16),
        ),
        in_specs=[pl.BlockSpec(memory_space=pltpu.VMEM)],
        out_specs=tuple(pl.BlockSpec(memory_space=pltpu.VMEM) for _ in range(3)),
        scratch_shapes=[
            pltpu.VMEM(square, jnp.float32),
            pltpu.VMEM((TILE, breadth), jnp.float32),
        ],
        cost_estimate=pl.CostEstimate(
            flops=8 * breadth**3, bytes_accessed=16 * breadth**2, transcendentals=0
        ),
        name="factor",
    )(packed)


def ortho_kernel(root_scale, own_at, in_at, kind, *refs):
    own, come = refs[:GROUP], refs[GROUP : 2 * GROUP]
    high_ref, low_ref, out_ref, block = refs[2 * GROUP :]
    step = pl.program_id(0)
    breadth = out_ref.shape[1]
    for g in range(GROUP):
        which = kind[step * GROUP + g]
        rows = pl.ds(g * TILE, TILE)

        @pl.when(which == 0)
        def _():
            block[rows, :] = jnp.zeros((TILE, breadth), block.dtype)

        @pl.when(which == 1)
        def _():
            block[rows, :] = own[g][...]

        @pl.when(which == 2)
        def _():
            block[rows, :] = come[g][...]

    for j in range(breadth // BIG):
        cols = slice(j * BIG, (j + 1) * BIG)
        width = (j + 1) * BIG
        left = block[:, :width]
        product = lax.dot_general(
            left, high_ref[cols, :width], NT, preferred_element_type=jnp.float32
        ) + lax.dot_general(left, low_ref[cols, :width], NT, preferred_element_type=jnp.float32)
        out_ref[:, cols] = (product * root_scale).astype(out_ref.dtype)


def carried(index, used):
    index = index.reshape(-1, GROUP)
    used = used.reshape(-1, GROUP)
    steps = jnp.arange(index.shape[0], dtype=jnp.int32)
    earlier = used[None, :, :] & (steps[None, :, None] <= steps[:, None, None])
    last = jnp.max(jnp.where(earlier, steps[None, :, None], -1), axis=1)
    pick = last[:, None, :] == steps[None, :, None]
    return jnp.sum(jnp.where(pick, index[None], 0), axis=1).reshape(-1)


def orthonormal(a_rows, received, own_at, in_at, kind, high, low, root_scale):
    breadth = a_rows.shape[1]
    rows = GROUP * TILE

    def own_spec(g):
        return pl.BlockSpec((TILE, breadth), lambda s, o, c, k: (o[s * GROUP + g], 0))

    def in_spec(g):
        return pl.BlockSpec((TILE, breadth), lambda s, o, c, k: (c[s * GROUP + g], 0))

    whole = pl.BlockSpec((breadth, breadth), lambda s, o, c, k: (0, 0))
    return pl.pallas_call(
        functools.partial(ortho_kernel, root_scale),
        out_shape=jax.ShapeDtypeStruct((SLOTS * TILE, breadth), a_rows.dtype),
        grid_spec=pltpu.PrefetchScalarGridSpec(
            num_scalar_prefetch=3,
            grid=(SLOTS // GROUP,),
            in_specs=[own_spec(g) for g in range(GROUP)]
            + [in_spec(g) for g in range(GROUP)]
            + [whole, whole],
            out_specs=pl.BlockSpec((rows, breadth), lambda s, o, c, k: (s, 0)),
            scratch_shapes=[pltpu.VMEM((rows, breadth), a_rows.dtype)],
        ),
        name="ortho",
    )(own_at, in_at, kind, *([a_rows] * GROUP), *([received] * GROUP), high, low)


def on_device(a_rows, heights, destination):
    breadth = a_rows.shape[1]
    size_gy = lax.axis_size("gy")
    devices = lax.axis_size("gx") * size_gy
    group_pos = lax.axis_index("gy")
    my_index = lax.axis_index("gx") * size_gy + group_pos
    group_base = my_index - group_pos
    tile_stack = a_rows.reshape(-1, TILE, breadth)
    stored = tile_stack.shape[0]
    tile_ids = jnp.arange(stored, dtype=jnp.int32)
    peer_ids = jnp.arange(size_gy, dtype=jnp.int32)
    slot_ids = jnp.arange(SLOTS, dtype=jnp.int32)
    tile_live = tile_ids[None, :] < heights[:, None]
    target_dev = destination // SLOTS
    target_slot = destination % SLOTS
    own_live = tile_live[group_pos]
    own_dev = target_dev[group_pos]
    own_slot = target_slot[group_pos]
    leaving = own_live & (own_dev != my_index)
    chosen = leaving[None, :] & (own_dev[None, :] - group_base == peer_ids[:, None])
    send_index = jnp.sum(jnp.where(chosen, tile_ids[None, :], 0), axis=1)
    arriving = tile_live & (target_dev == my_index) & (peer_ids[:, None] != group_pos)
    arrive_slot = jnp.sum(jnp.where(arriving, target_slot, 0), axis=1)
    arrive_has = jnp.any(arriving, axis=1)
    staying = own_live & (own_dev == my_index)
    own_match = staying[None, :] & (own_slot[None, :] == slot_ids[:, None])
    in_match = arrive_has[None, :] & (arrive_slot[None, :] == slot_ids[:, None])
    own_has = jnp.any(own_match, axis=1)
    in_has = jnp.any(in_match, axis=1)
    own_at = carried(jnp.sum(jnp.where(own_match, tile_ids[None, :], 0), axis=1), own_has)
    in_at = carried(jnp.sum(jnp.where(in_match, peer_ids[None, :], 0), axis=1), in_has)
    kind = jnp.where(own_has, 1, jnp.where(in_has, 2, 0)).astype(jnp.int32)
    root_scale = math.sqrt(devices * SLOTS * TILE)
    sizes = grid_sizes()
    packed = local_gram(a_rows, lax.dynamic_slice(heights, (group_pos,), (1,)), 2 * devices)
    packed = reduce_all(packed, sizes)
    packed, outgoing = lax.optimization_barrier((packed, tile_stack[send_index]))
    received = lax.all_to_all(
        outgoing, "gy", split_axis=0, concat_axis=0, tiled=True
    ).reshape(-1, breadth)
    factor_r, high, low = factor(packed, breadth, root_scale)
    ortho_rows = orthonormal(a_rows, received, own_at, in_at, kind, high, low, root_scale)
    return (ortho_rows, factor_r)


def solution(mesh):
    placed = (P(("gx", "gy"), None), P("gx"), P("gx", None))
    return jax.shard_map(
        on_device,
        mesh=mesh,
        in_specs=placed,
        out_specs=(P(("gx", "gy"), None), P()),
        check_vma=False,
    )
```

```python
import functools
import math

import jax
import jax.numpy as jnp
from jax import lax
from jax.experimental import pallas as pl
from jax.experimental.pallas import tpu as pltpu
from jax.sharding import PartitionSpec as P

TILE = 128
SLOTS = 32
GROUP = 4
BIG = 256
PANEL = 8
REGS = TILE // 8
STREAMS = 6
NT = (((1,), (1,)), ((), ()))


def gram_kernel(height_ref, sent_at, a_ref, *refs):
    sent, out_ref, packed_ref = refs[:-2], refs[-2], refs[-1]
    for g, tile in enumerate(sent):
        packed_ref[g * TILE : (g + 1) * TILE, :] = tile[...]
    step = pl.program_id(0)
    rows, breadth = a_ref.shape
    live = height_ref[0] * TILE - step * rows

    @pl.when(step == 0)
    def _():
        out_ref[...] = jnp.zeros_like(out_ref)

    def add(block):
        across = block.T
        place = 0
        for i in range(0, breadth, BIG):
            product = jnp.dot(
                across[i : i + BIG], block[:, i:], preferred_element_type=jnp.float32
            )
            for top in range(0, BIG, TILE):
                for j in range(top, breadth - i, TILE):
                    piece = product[top : top + TILE, j : j + TILE]
                    out_ref[place : place + REGS] += piece.reshape(REGS, 8, TILE)
                    place += REGS

    @pl.when(live >= rows)
    def _():
        add(a_ref[...])

    @pl.when((live > 0) & (live < rows))
    def _():
        index = lax.broadcasted_iota(jnp.int32, (rows, breadth), 0)
        keep = (index < live).astype(jnp.float32).astype(a_ref.dtype)
        add(a_ref[...] * keep)


def local_gram(a_rows, height, send_index, split):
    total, breadth = a_rows.shape
    rows = GROUP * TILE
    blocks = breadth // TILE
    packed = pl.cdiv(blocks * (blocks + 1) // 2 * REGS, split) * split
    steps = total // rows
    peers = send_index.shape[0]
    each = 1
    while each * steps < peers or peers % each:
        each += 1
    last = peers // each - 1

    def sent_spec(g):
        return pl.BlockSpec(
            (TILE, breadth), lambda i, h, t: (t[jnp.minimum(i, last) * each + g], 0)
        )

    return pl.pallas_call(
        gram_kernel,
        out_shape=(
            jax.ShapeDtypeStruct((packed, 8, TILE), jnp.float32),
            jax.ShapeDtypeStruct((peers * TILE, breadth), a_rows.dtype),
        ),
        grid_spec=pltpu.PrefetchScalarGridSpec(
            num_scalar_prefetch=2,
            grid=(steps,),
            in_specs=[
                pl.BlockSpec(
                    (rows, breadth),
                    lambda i, h, t: (jnp.minimum(i, (h[0] - 1) // GROUP), 0),
                )
            ]
            + [sent_spec(g) for g in range(each)],
            out_specs=(
                pl.BlockSpec((packed, 8, TILE), lambda i, h, t: (0, 0, 0)),
                pl.BlockSpec((each * TILE, breadth), lambda i, h, t: (jnp.minimum(i, last), 0)),
            ),
        ),
        cost_estimate=pl.CostEstimate(
            flops=total * breadth * breadth, bytes_accessed=total * breadth * 2, transcendentals=0
        ),
        name="gram",
    )(height, send_index, a_rows, *([a_rows] * each))


def eliminate(block):
    lane = lax.broadcasted_iota(jnp.int32, (1, TILE), 1)
    sub = lax.broadcasted_iota(jnp.int32, (8, TILE), 0)
    parts = [block[8 * g : 8 * g + 8] for g in range(TILE // 8)]
    for first in range(0, TILE, PANEL):
        start = first // 8
        spread = [
            [jnp.broadcast_to(part[:, first + m : first + m + 1], (8, TILE)) for part in parts[start:]]
            for m in range(PANEL)
        ]
        for m in range(PANEL):
            at = first + m
            home, local = at // 8, at % 8
            skip = home - start
            column = spread[m]
            pivot = jnp.broadcast_to(column[skip][local : local + 1], (8, TILE))
            inverse = 1.0 / pivot
            below = sub > local
            factors = [c * inverse for c in column[skip:]]
            factors[0] = jnp.where(below, factors[0], 0.0)
            here = lane == at
            row = jnp.where(here, 1.0, parts[home][local : local + 1])
            row = jnp.broadcast_to(row, (8, TILE))
            for n in range(m + 1, PANEL):
                level = jnp.broadcast_to(spread[n][skip][local : local + 1], (8, TILE))
                spread[n] = spread[n][:skip] + [
                    c - f * level for c, f in zip(spread[n][skip:], factors)
                ]
            for g in range(home, len(parts)):
                clear = here & below if g == home else here
                parts[g] = jnp.where(clear, 0.0, parts[g]) - factors[g - home] * row
    return jnp.concatenate(parts, axis=0)


def thirds(value):
    first = value.astype(jnp.bfloat16)
    rest = value - first.astype(jnp.float32)
    second = rest.astype(jnp.bfloat16)
    third = (rest - second.astype(jnp.float32)).astype(jnp.bfloat16)
    return first, second, third


def left_terms(value):
    first, second, third = thirds(value)
    return jnp.concatenate([first, first, second, second, first, third], axis=1)


def right_terms(value):
    first, second, third = thirds(value)
    return jnp.concatenate([first, second, first, second, third, first], axis=0)


def factor_kernel(root_scale, gram_ref, r_ref, high_ref, low_ref, work, line, left, right):
    breadth = r_ref.shape[0]
    count = breadth // TILE
    place = 0
    for i in range(count):
        for j in range(i, count):
            block = gram_ref[place : place + REGS].reshape(TILE, TILE)
            work[i * TILE : (i + 1) * TILE, j * TILE : (j + 1) * TILE] = block
            place += REGS
    rows_id = lax.broadcasted_iota(jnp.int32, (TILE, TILE), 0)
    cols_id = lax.broadcasted_iota(jnp.int32, (TILE, TILE), 1)
    wide_id = lax.broadcasted_iota(jnp.int32, (TILE, breadth), 1)

    def step(k, carry):
        base = pl.multiple_of(k * TILE, TILE)
        mine = pl.ds(base, TILE)
        right[...] = right_terms(work[mine, :])
        done = eliminate(work[mine, mine])
        diagonal = jnp.sum(jnp.where(rows_id == cols_id, done, 0.0), axis=1, keepdims=True)
        shrink = 1.0 / jnp.sqrt(diagonal)
        inverse = jnp.where(
            rows_id > cols_id, done, jnp.where(rows_id == cols_id, 1.0, 0.0)
        ) * shrink
        upper = jnp.where(rows_id <= cols_id, done, 0.0) * shrink
        line[...] = jnp.dot(
            left_terms(inverse), right[...], preferred_element_type=jnp.float32
        )
        r_ref[mine, :] = jnp.where(wide_id >= base, line[...], 0.0) * (1.0 / root_scale)
        r_ref[mine, mine] = upper * (1.0 / root_scale)
        line[:, mine] = inverse
        solved = jnp.where(wide_id < base + TILE, line[...], 0.0)
        high = solved.astype(jnp.bfloat16)
        high_ref[mine, :] = high
        low_ref[mine, :] = (solved - high.astype(jnp.float32)).astype(jnp.bfloat16)

        @pl.when(k + 1 < count)
        def _():
            later = jnp.where(wide_id >= base + TILE, line[...], 0.0)
            left[...] = left_terms(later.T)
            right[...] = right_terms(line[...])

            def update(i, carry):
                theirs = pl.ds(pl.multiple_of(i * BIG, BIG), BIG)
                work[theirs, mine] = jnp.zeros((BIG, TILE), jnp.float32)
                work[theirs, :] -= jnp.dot(
                    left[theirs, :], right[...], preferred_element_type=jnp.float32
                )
                return carry

            lax.fori_loop((k + 1) * TILE // BIG, breadth // BIG, update, 0)

        return carry

    lax.fori_loop(0, count, step, 0)


def stream_orders():
    return (("core", "x", "y", "z"), ("core", "y", "x", "z")) * (STREAMS // 2)


def reduce_kernel(sizes, x_ref, out_ref, work, *rest):
    streams = stream_orders()
    count = len(streams)
    depth = len(streams[0])
    arrived, sends, recvs = rest[: count * depth], rest[count * depth], rest[count * depth + 1]
    at_gx, at_gy = lax.axis_index("gx"), lax.axis_index("gy")
    pair, across = sizes["core"], sizes["x"]
    here = {
        "core": lax.rem(at_gx, pair),
        "y": lax.div(at_gx, pair),
        "x": lax.rem(at_gy, across),
        "z": lax.div(at_gy, across),
    }

    def peer(dim, offset):
        there = dict(here)
        there[dim] = lax.rem(here[dim] + offset, sizes[dim])
        where = (there["y"] * pair + there["core"], there["z"] * across + there["x"])
        return there[dim], where

    barrier = pltpu.get_barrier_semaphore()
    greeted = 0
    for dim in streams[0]:
        for offset in range(1, sizes[dim]):
            pl.semaphore_signal(
                barrier, inc=1, device_id=peer(dim, offset)[1], device_id_type=pl.DeviceIdType.MESH
            )
            greeted += 1
    pl.semaphore_wait(barrier, greeted)

    share = x_ref.shape[0] // count
    used = [0]

    def send(source, target, where):
        slot = used[0]
        used[0] += 1
        copy = pltpu.make_async_remote_copy(
            src_ref=source,
            dst_ref=target,
            send_sem=sends.at[slot],
            recv_sem=recvs.at[slot],
            device_id=where,
            device_id_type=pl.DeviceIdType.MESH,
        )
        copy.start()
        return copy

    pending = []
    base = [share * s for s in range(count)]
    size = [share] * count
    bases = [[] for _ in range(count)]

    def scatter(s, level):
        dim = streams[s][level]
        part = size[s] // sizes[dim]
        source = x_ref if level == 0 else work
        copies = []
        for offset in range(1, sizes[dim]):
            index, where = peer(dim, offset)
            copies.append(
                send(
                    source.at[pl.ds(base[s] + index * part, part)],
                    arrived[s * depth + level].at[offset - 1],
                    where,
                )
            )
        return copies

    def collect(s, level, copies):
        dim = streams[s][level]
        part = size[s] // sizes[dim]
        source = x_ref if level == 0 else work
        target = out_ref if level == depth - 1 else work
        mine = pl.ds(base[s] + here[dim] * part, part)
        for copy in copies:
            copy.wait_recv()
        total = source[mine]
        for offset in range(1, sizes[dim]):
            total += arrived[s * depth + level][offset - 1]
        target[mine] = total
        pending.extend(copies)
        base[s] = base[s] + here[dim] * part
        size[s] = part
        bases[s].append((base[s], part))

    def gather(s, level):
        start, part = bases[s][level]
        dim = streams[s][level]
        mine = out_ref.at[pl.ds(start, part)]
        return [send(mine, mine, peer(dim, offset)[1]) for offset in range(1, sizes[dim])]

    def landed(copies):
        for copy in copies:
            copy.wait_recv()
        pending.extend(copies)

    flying = [scatter(s, 0) for s in range(count)]
    for wave in range(2 * depth + count // 2 - 1):
        for s in range(count):
            stage = wave - s // 2
            if 0 <= stage < depth:
                collect(s, stage, flying[s])
                flying[s] = scatter(s, stage + 1) if stage + 1 < depth else gather(s, stage)
            elif depth <= stage < 2 * depth:
                landed(flying[s])
                if stage + 1 < 2 * depth:
                    flying[s] = gather(s, 2 * depth - 2 - stage)
    for copy in pending:
        copy.wait_send()


def grid_sizes():
    size_gx, size_gy = lax.axis_size("gx"), lax.axis_size("gy")
    across = 1
    while across * across * 4 <= size_gy and size_gy % (across * 2) == 0:
        across *= 2
    pair = 2 if size_gx % 2 == 0 else 1
    return {"core": pair, "y": size_gx // pair, "x": across, "z": size_gy // across}


def reduce_all(packed, sizes):
    part = packed.shape[0] // STREAMS
    buffers = []
    for order in stream_orders():
        left = part
        for dim in order:
            left //= sizes[dim]
            buffers.append(pltpu.VMEM((max(sizes[dim] - 1, 1), left, 8, TILE), jnp.float32))
    copies = 2 * STREAMS * sum(n - 1 for n in sizes.values())
    return pl.pallas_call(
        functools.partial(reduce_kernel, sizes),
        out_shape=jax.ShapeDtypeStruct(packed.shape, jnp.float32),
        in_specs=[pl.BlockSpec(memory_space=pltpu.VMEM)],
        out_specs=pl.BlockSpec(memory_space=pltpu.VMEM),
        scratch_shapes=[pltpu.VMEM(packed.shape, jnp.float32)]
        + buffers
        + [pltpu.SemaphoreType.DMA((copies,)), pltpu.SemaphoreType.DMA((copies,))],
        compiler_params=pltpu.CompilerParams(collective_id=0, has_side_effects=True),
        name="reduce_all",
    )(packed)


def factor(packed, breadth, root_scale):
    square = (breadth, breadth)
    return pl.pallas_call(
        functools.partial(factor_kernel, root_scale),
        out_shape=(
            jax.ShapeDtypeStruct(square, jnp.float32),
            jax.ShapeDtypeStruct(square, jnp.bfloat16),
            jax.ShapeDtypeStruct(square, jnp.bfloat16),
        ),
        in_specs=[pl.BlockSpec(memory_space=pltpu.VMEM)],
        out_specs=tuple(pl.BlockSpec(memory_space=pltpu.VMEM) for _ in range(3)),
        scratch_shapes=[
            pltpu.VMEM(square, jnp.float32),
            pltpu.VMEM((TILE, breadth), jnp.float32),
            pltpu.VMEM((breadth, 6 * TILE), jnp.bfloat16),
            pltpu.VMEM((6 * TILE, breadth), jnp.bfloat16),
        ],
        cost_estimate=pl.CostEstimate(
            flops=8 * breadth**3, bytes_accessed=16 * breadth**2, transcendentals=0
        ),
        name="factor",
    )(packed)


def ortho_kernel(root_scale, own_at, in_at, kind, *refs):
    own, come = refs[:GROUP], refs[GROUP : 2 * GROUP]
    high_ref, low_ref, out_ref, block = refs[2 * GROUP :]
    step = pl.program_id(0)
    breadth = out_ref.shape[1]
    for g in range(GROUP):
        which = kind[step * GROUP + g]
        rows = pl.ds(g * TILE, TILE)

        @pl.when(which == 0)
        def _():
            block[rows, :] = jnp.zeros((TILE, breadth), block.dtype)

        @pl.when(which == 1)
        def _():
            block[rows, :] = own[g][...]

        @pl.when(which == 2)
        def _():
            block[rows, :] = come[g][...]

    for j in range(breadth // BIG):
        cols = slice(j * BIG, (j + 1) * BIG)
        width = (j + 1) * BIG
        left = block[:, :width]
        product = lax.dot_general(
            left, high_ref[cols, :width], NT, preferred_element_type=jnp.float32
        ) + lax.dot_general(left, low_ref[cols, :width], NT, preferred_element_type=jnp.float32)
        out_ref[:, cols] = (product * root_scale).astype(out_ref.dtype)


def carried(index, used):
    index = index.reshape(-1, GROUP)
    used = used.reshape(-1, GROUP)
    steps = jnp.arange(index.shape[0], dtype=jnp.int32)
    earlier = used[None, :, :] & (steps[None, :, None] <= steps[:, None, None])
    last = jnp.max(jnp.where(earlier, steps[None, :, None], -1), axis=1)
    pick = last[:, None, :] == steps[None, :, None]
    return jnp.sum(jnp.where(pick, index[None], 0), axis=1).reshape(-1)


def orthonormal(a_rows, received, own_at, in_at, kind, high, low, root_scale):
    breadth = a_rows.shape[1]
    rows = GROUP * TILE

    def own_spec(g):
        return pl.BlockSpec((TILE, breadth), lambda s, o, c, k: (o[s * GROUP + g], 0))

    def in_spec(g):
        return pl.BlockSpec((TILE, breadth), lambda s, o, c, k: (c[s * GROUP + g], 0))

    whole = pl.BlockSpec((breadth, breadth), lambda s, o, c, k: (0, 0))
    return pl.pallas_call(
        functools.partial(ortho_kernel, root_scale),
        out_shape=jax.ShapeDtypeStruct((SLOTS * TILE, breadth), a_rows.dtype),
        grid_spec=pltpu.PrefetchScalarGridSpec(
            num_scalar_prefetch=3,
            grid=(SLOTS // GROUP,),
            in_specs=[own_spec(g) for g in range(GROUP)]
            + [in_spec(g) for g in range(GROUP)]
            + [whole, whole],
            out_specs=pl.BlockSpec((rows, breadth), lambda s, o, c, k: (s, 0)),
            scratch_shapes=[pltpu.VMEM((rows, breadth), a_rows.dtype)],
        ),
        name="ortho",
    )(own_at, in_at, kind, *([a_rows] * GROUP), *([received] * GROUP), high, low)


def on_device(a_rows, heights, destination):
    breadth = a_rows.shape[1]
    size_gy = lax.axis_size("gy")
    devices = lax.axis_size("gx") * size_gy
    group_pos = lax.axis_index("gy")
    my_index = lax.axis_index("gx") * size_gy + group_pos
    group_base = my_index - group_pos
    stored = a_rows.shape[0] // TILE
    tile_ids = jnp.arange(stored, dtype=jnp.int32)
    peer_ids = jnp.arange(size_gy, dtype=jnp.int32)
    slot_ids = jnp.arange(SLOTS, dtype=jnp.int32)
    tile_live = tile_ids[None, :] < heights[:, None]
    target_dev = destination // SLOTS
    target_slot = destination % SLOTS
    own_live = tile_live[group_pos]
    own_dev = target_dev[group_pos]
    own_slot = target_slot[group_pos]
    leaving = own_live & (own_dev != my_index)
    chosen = leaving[None, :] & (own_dev[None, :] - group_base == peer_ids[:, None])
    send_index = jnp.sum(jnp.where(chosen, tile_ids[None, :], 0), axis=1)
    arriving = tile_live & (target_dev == my_index) & (peer_ids[:, None] != group_pos)
    arrive_slot = jnp.sum(jnp.where(arriving, target_slot, 0), axis=1)
    arrive_has = jnp.any(arriving, axis=1)
    staying = own_live & (own_dev == my_index)
    own_match = staying[None, :] & (own_slot[None, :] == slot_ids[:, None])
    in_match = arrive_has[None, :] & (arrive_slot[None, :] == slot_ids[:, None])
    own_has = jnp.any(own_match, axis=1)
    in_has = jnp.any(in_match, axis=1)
    own_at = carried(jnp.sum(jnp.where(own_match, tile_ids[None, :], 0), axis=1), own_has)
    in_at = carried(jnp.sum(jnp.where(in_match, peer_ids[None, :], 0), axis=1), in_has)
    kind = jnp.where(own_has, 1, jnp.where(in_has, 2, 0)).astype(jnp.int32)
    root_scale = math.sqrt(devices * SLOTS * TILE)
    sizes = grid_sizes()
    height = lax.dynamic_slice(heights, (group_pos,), (1,))
    packed, outgoing = local_gram(a_rows, height, send_index, STREAMS * devices)
    packed = reduce_all(packed, sizes)
    packed, outgoing = lax.optimization_barrier((packed, outgoing))
    received = lax.all_to_all(
        outgoing.reshape(-1, TILE, breadth), "gy", split_axis=0, concat_axis=0, tiled=True
    ).reshape(-1, breadth)
    factor_r, high, low = factor(packed, breadth, root_scale)
    ortho_rows = orthonormal(a_rows, received, own_at, in_at, kind, high, low, root_scale)
    return (ortho_rows, factor_r)


def solution(mesh):
    placed = (P(("gx", "gy"), None), P("gx"), P("gx", None))
    return jax.shard_map(
        on_device,
        mesh=mesh,
        in_specs=placed,
        out_specs=(P(("gx", "gy"), None), P()),
        check_vma=False,
    )
```

```python
import functools
import math

import jax
import jax.numpy as jnp
from jax import lax
from jax.experimental import pallas as pl
from jax.experimental.pallas import tpu as pltpu
from jax.sharding import PartitionSpec as P

TILE = 128
SLOTS = 32
GROUP = 4
BIG = 256
PANEL = 8
REGS = TILE // 8
STREAMS = 6
NT = (((1,), (1,)), ((), ()))


def gram_kernel(height_ref, sent_at, a_ref, *refs):
    sent, out_ref, packed_ref = refs[:-2], refs[-2], refs[-1]
    for g, tile in enumerate(sent):
        packed_ref[g * TILE : (g + 1) * TILE, :] = tile[...]
    step = pl.program_id(0)
    rows, breadth = a_ref.shape
    live = height_ref[0] * TILE - step * rows

    @pl.when(step == 0)
    def _():
        out_ref[...] = jnp.zeros_like(out_ref)

    def add(block):
        across = block.T
        place = 0
        for i in range(0, breadth, BIG):
            product = jnp.dot(
                across[i : i + BIG], block[:, i:], preferred_element_type=jnp.float32
            )
            for top in range(0, BIG, TILE):
                for j in range(top, breadth - i, TILE):
                    piece = product[top : top + TILE, j : j + TILE]
                    out_ref[place : place + REGS] += piece.reshape(REGS, 8, TILE)
                    place += REGS

    @pl.when(live >= rows)
    def _():
        add(a_ref[...])

    @pl.when((live > 0) & (live < rows))
    def _():
        index = lax.broadcasted_iota(jnp.int32, (rows, breadth), 0)
        keep = (index < live).astype(jnp.float32).astype(a_ref.dtype)
        add(a_ref[...] * keep)


def local_gram(a_rows, height, send_index, split):
    total, breadth = a_rows.shape
    rows = GROUP * TILE
    blocks = breadth // TILE
    packed = pl.cdiv(blocks * (blocks + 1) // 2 * REGS, split) * split
    steps = total // rows
    peers = send_index.shape[0]
    each = 1
    while each * steps < peers or peers % each:
        each += 1
    last = peers // each - 1

    def sent_spec(g):
        return pl.BlockSpec(
            (TILE, breadth), lambda i, h, t: (t[jnp.minimum(i, last) * each + g], 0)
        )

    return pl.pallas_call(
        gram_kernel,
        out_shape=(
            jax.ShapeDtypeStruct((packed, 8, TILE), jnp.float32),
            jax.ShapeDtypeStruct((peers * TILE, breadth), a_rows.dtype),
        ),
        grid_spec=pltpu.PrefetchScalarGridSpec(
            num_scalar_prefetch=2,
            grid=(steps,),
            in_specs=[
                pl.BlockSpec(
                    (rows, breadth),
                    lambda i, h, t: (jnp.minimum(i, (h[0] - 1) // GROUP), 0),
                )
            ]
            + [sent_spec(g) for g in range(each)],
            out_specs=(
                pl.BlockSpec((packed, 8, TILE), lambda i, h, t: (0, 0, 0)),
                pl.BlockSpec((each * TILE, breadth), lambda i, h, t: (jnp.minimum(i, last), 0)),
            ),
        ),
        cost_estimate=pl.CostEstimate(
            flops=total * breadth * breadth, bytes_accessed=total * breadth * 2, transcendentals=0
        ),
        name="gram",
    )(height, send_index, a_rows, *([a_rows] * each))


def eliminate(block):
    lane = lax.broadcasted_iota(jnp.int32, (1, TILE), 1)
    sub = lax.broadcasted_iota(jnp.int32, (8, TILE), 0)
    parts = [block[8 * g : 8 * g + 8] for g in range(TILE // 8)]
    for first in range(0, TILE, PANEL):
        start = first // 8
        spread = [
            [jnp.broadcast_to(part[:, first + m : first + m + 1], (8, TILE)) for part in parts[start:]]
            for m in range(PANEL)
        ]
        for m in range(PANEL):
            at = first + m
            home, local = at // 8, at % 8
            skip = home - start
            column = spread[m]
            pivot = jnp.broadcast_to(column[skip][local : local + 1], (8, TILE))
            inverse = 1.0 / pivot
            below = sub > local
            factors = [c * inverse for c in column[skip:]]
            factors[0] = jnp.where(below, factors[0], 0.0)
            here = lane == at
            row = jnp.where(here, 1.0, parts[home][local : local + 1])
            row = jnp.broadcast_to(row, (8, TILE))
            for n in range(m + 1, PANEL):
                level = jnp.broadcast_to(spread[n][skip][local : local + 1], (8, TILE))
                spread[n] = spread[n][:skip] + [
                    c - f * level for c, f in zip(spread[n][skip:], factors)
                ]
            for g in range(home, len(parts)):
                clear = here & below if g == home else here
                parts[g] = jnp.where(clear, 0.0, parts[g]) - factors[g - home] * row
    return jnp.concatenate(parts, axis=0)


def thirds(value):
    first = value.astype(jnp.bfloat16)
    rest = value - first.astype(jnp.float32)
    second = rest.astype(jnp.bfloat16)
    third = (rest - second.astype(jnp.float32)).astype(jnp.bfloat16)
    return first, second, third


def left_terms(value):
    first, second, third = thirds(value)
    return jnp.concatenate([first, first, second, second, first, third], axis=1)


def right_terms(value):
    first, second, third = thirds(value)
    return jnp.concatenate([first, second, first, second, third, first], axis=0)


def factor_kernel(root_scale, gram_ref, r_ref, high_ref, low_ref, work, line, left, right):
    breadth = r_ref.shape[0]
    count = breadth // TILE
    place = 0
    for i in range(count):
        for j in range(i, count):
            block = gram_ref[place : place + REGS].reshape(TILE, TILE)
            work[i * TILE : (i + 1) * TILE, j * TILE : (j + 1) * TILE] = block
            place += REGS
    rows_id = lax.broadcasted_iota(jnp.int32, (TILE, TILE), 0)
    cols_id = lax.broadcasted_iota(jnp.int32, (TILE, TILE), 1)
    wide_id = lax.broadcasted_iota(jnp.int32, (TILE, breadth), 1)

    def step(k, carry):
        base = pl.multiple_of(k * TILE, TILE)
        mine = pl.ds(base, TILE)
        right[...] = right_terms(work[mine, :])
        done = eliminate(work[mine, mine])
        diagonal = jnp.sum(jnp.where(rows_id == cols_id, done, 0.0), axis=1, keepdims=True)
        shrink = 1.0 / jnp.sqrt(diagonal)
        inverse = jnp.where(
            rows_id > cols_id, done, jnp.where(rows_id == cols_id, 1.0, 0.0)
        ) * shrink
        upper = jnp.where(rows_id <= cols_id, done, 0.0) * shrink
        line[...] = jnp.dot(
            left_terms(inverse), right[...], preferred_element_type=jnp.float32
        )
        r_ref[mine, :] = jnp.where(wide_id >= base, line[...], 0.0) * (1.0 / root_scale)
        r_ref[mine, mine] = upper * (1.0 / root_scale)
        line[:, mine] = inverse
        solved = jnp.where(wide_id < base + TILE, line[...], 0.0)
        high = solved.astype(jnp.bfloat16)
        high_ref[mine, :] = high
        low_ref[mine, :] = (solved - high.astype(jnp.float32)).astype(jnp.bfloat16)

        @pl.when(k + 1 < count)
        def _():
            later = jnp.where(wide_id >= base + TILE, line[...], 0.0)
            left[...] = left_terms(later.T)
            right[...] = right_terms(line[...])

            def update(i, carry):
                theirs = pl.ds(pl.multiple_of(i * BIG, BIG), BIG)
                work[theirs, mine] = jnp.zeros((BIG, TILE), jnp.float32)
                work[theirs, :] -= jnp.dot(
                    left[theirs, :], right[...], preferred_element_type=jnp.float32
                )
                return carry

            lax.fori_loop((k + 1) * TILE // BIG, breadth // BIG, update, 0)

        return carry

    lax.fori_loop(0, count, step, 0)


def stream_orders():
    return (("core", "x", "y", "z"), ("core", "y", "x", "z")) * (STREAMS // 2)


def reduce_kernel(sizes, x_ref, out_ref, work, *rest):
    streams = stream_orders()
    count = len(streams)
    depth = len(streams[0])
    arrived, sends, recvs = rest[: count * depth], rest[count * depth], rest[count * depth + 1]
    at_gx, at_gy = lax.axis_index("gx"), lax.axis_index("gy")
    pair, across = sizes["core"], sizes["x"]
    here = {
        "core": lax.rem(at_gx, pair),
        "y": lax.div(at_gx, pair),
        "x": lax.rem(at_gy, across),
        "z": lax.div(at_gy, across),
    }

    def peer(dim, offset):
        there = dict(here)
        there[dim] = lax.rem(here[dim] + offset, sizes[dim])
        where = (there["y"] * pair + there["core"], there["z"] * across + there["x"])
        return there[dim], where

    barrier = pltpu.get_barrier_semaphore()
    greeted = 0
    for dim in streams[0]:
        for offset in range(1, sizes[dim]):
            pl.semaphore_signal(
                barrier, inc=1, device_id=peer(dim, offset)[1], device_id_type=pl.DeviceIdType.MESH
            )
            greeted += 1
    pl.semaphore_wait(barrier, greeted)

    share = x_ref.shape[0] // count
    used = [0]

    def send(source, target, where):
        slot = used[0]
        used[0] += 1
        copy = pltpu.make_async_remote_copy(
            src_ref=source,
            dst_ref=target,
            send_sem=sends.at[slot],
            recv_sem=recvs.at[slot],
            device_id=where,
            device_id_type=pl.DeviceIdType.MESH,
        )
        copy.start()
        return copy

    pending = []
    base = [share * s for s in range(count)]
    size = [share] * count
    bases = [[] for _ in range(count)]

    def scatter(s, level):
        dim = streams[s][level]
        part = size[s] // sizes[dim]
        source = x_ref if level == 0 else work
        copies = []
        for offset in range(1, sizes[dim]):
            index, where = peer(dim, offset)
            copies.append(
                send(
                    source.at[pl.ds(base[s] + index * part, part)],
                    arrived[s * depth + level].at[offset - 1],
                    where,
                )
            )
        return copies

    def collect(s, level, copies):
        dim = streams[s][level]
        part = size[s] // sizes[dim]
        source = x_ref if level == 0 else work
        target = out_ref if level == depth - 1 else work
        mine = pl.ds(base[s] + here[dim] * part, part)
        for copy in copies:
            copy.wait_recv()
        total = source[mine]
        for offset in range(1, sizes[dim]):
            total += arrived[s * depth + level][offset - 1]
        target[mine] = total
        pending.extend(copies)
        base[s] = base[s] + here[dim] * part
        size[s] = part
        bases[s].append((base[s], part))

    def gather(s, level):
        start, part = bases[s][level]
        dim = streams[s][level]
        mine = out_ref.at[pl.ds(start, part)]
        return [send(mine, mine, peer(dim, offset)[1]) for offset in range(1, sizes[dim])]

    def landed(copies):
        for copy in copies:
            copy.wait_recv()
        pending.extend(copies)

    flying = [scatter(s, 0) for s in range(count)]
    for wave in range(2 * depth + count // 2 - 1):
        for s in range(count):
            stage = wave - s // 2
            if 0 <= stage < depth:
                collect(s, stage, flying[s])
                flying[s] = scatter(s, stage + 1) if stage + 1 < depth else gather(s, stage)
            elif depth <= stage < 2 * depth:
                landed(flying[s])
                if stage + 1 < 2 * depth:
                    flying[s] = gather(s, 2 * depth - 2 - stage)
    for copy in pending:
        copy.wait_send()


def grid_sizes():
    size_gx, size_gy = lax.axis_size("gx"), lax.axis_size("gy")
    across = 1
    while across * across * 4 <= size_gy and size_gy % (across * 2) == 0:
        across *= 2
    pair = 2 if size_gx % 2 == 0 else 1
    return {"core": pair, "y": size_gx // pair, "x": across, "z": size_gy // across}


def reduce_all(packed, sizes):
    part = packed.shape[0] // STREAMS
    buffers = []
    for order in stream_orders():
        left = part
        for dim in order:
            left //= sizes[dim]
            buffers.append(pltpu.VMEM((max(sizes[dim] - 1, 1), left, 8, TILE), jnp.float32))
    copies = 2 * STREAMS * sum(n - 1 for n in sizes.values())
    return pl.pallas_call(
        functools.partial(reduce_kernel, sizes),
        out_shape=jax.ShapeDtypeStruct(packed.shape, jnp.float32),
        in_specs=[pl.BlockSpec(memory_space=pltpu.VMEM)],
        out_specs=pl.BlockSpec(memory_space=pltpu.VMEM),
        scratch_shapes=[pltpu.VMEM(packed.shape, jnp.float32)]
        + buffers
        + [pltpu.SemaphoreType.DMA((copies,)), pltpu.SemaphoreType.DMA((copies,))],
        compiler_params=pltpu.CompilerParams(collective_id=0, has_side_effects=True),
        name="reduce_all",
    )(packed)


def factor(packed, breadth, root_scale):
    square = (breadth, breadth)
    return pl.pallas_call(
        functools.partial(factor_kernel, root_scale),
        out_shape=(
            jax.ShapeDtypeStruct(square, jnp.float32),
            jax.ShapeDtypeStruct(square, jnp.bfloat16),
            jax.ShapeDtypeStruct(square, jnp.bfloat16),
        ),
        in_specs=[pl.BlockSpec(memory_space=pltpu.VMEM)],
        out_specs=tuple(pl.BlockSpec(memory_space=pltpu.VMEM) for _ in range(3)),
        scratch_shapes=[
            pltpu.VMEM(square, jnp.float32),
            pltpu.VMEM((TILE, breadth), jnp.float32),
            pltpu.VMEM((breadth, 6 * TILE), jnp.bfloat16),
            pltpu.VMEM((6 * TILE, breadth), jnp.bfloat16),
        ],
        cost_estimate=pl.CostEstimate(
            flops=8 * breadth**3, bytes_accessed=16 * breadth**2, transcendentals=0
        ),
        name="factor",
    )(packed)


def ortho_kernel(root_scale, own_at, in_at, kind, *refs):
    own, come = refs[:GROUP], refs[GROUP : 2 * GROUP]
    high_ref, low_ref, out_ref, block = refs[2 * GROUP :]
    step = pl.program_id(0)
    breadth = out_ref.shape[1]
    for g in range(GROUP):
        which = kind[step * GROUP + g]
        rows = pl.ds(g * TILE, TILE)

        @pl.when(which == 0)
        def _():
            block[rows, :] = jnp.zeros((TILE, breadth), block.dtype)

        @pl.when(which == 1)
        def _():
            block[rows, :] = own[g][...]

        @pl.when(which == 2)
        def _():
            block[rows, :] = come[g][...]

    for j in range(breadth // BIG):
        cols = slice(j * BIG, (j + 1) * BIG)
        width = (j + 1) * BIG
        left = block[:, :width]
        product = lax.dot_general(
            left, high_ref[cols, :width], NT, preferred_element_type=jnp.float32
        ) + lax.dot_general(left, low_ref[cols, :width], NT, preferred_element_type=jnp.float32)
        out_ref[:, cols] = (product * root_scale).astype(out_ref.dtype)


def carried(index, used):
    slots = jnp.arange(index.shape[0], dtype=jnp.int32)
    lanes = slots % GROUP
    earlier = used[None, :] & (slots[None, :] <= slots[:, None]) & (lanes[None, :] == lanes[:, None])
    last = jnp.max(jnp.where(earlier, slots[None, :], -1), axis=1)
    return jnp.sum(jnp.where(last[:, None] == slots[None, :], index[None, :], 0), axis=1)


def orthonormal(a_rows, received, own_at, in_at, kind, high, low, root_scale):
    breadth = a_rows.shape[1]
    rows = GROUP * TILE

    def own_spec(g):
        return pl.BlockSpec((TILE, breadth), lambda s, o, c, k: (o[s * GROUP + g], 0))

    def in_spec(g):
        return pl.BlockSpec((TILE, breadth), lambda s, o, c, k: (c[s * GROUP + g], 0))

    whole = pl.BlockSpec((breadth, breadth), lambda s, o, c, k: (0, 0))
    return pl.pallas_call(
        functools.partial(ortho_kernel, root_scale),
        out_shape=jax.ShapeDtypeStruct((SLOTS * TILE, breadth), a_rows.dtype),
        grid_spec=pltpu.PrefetchScalarGridSpec(
            num_scalar_prefetch=3,
            grid=(SLOTS // GROUP,),
            in_specs=[own_spec(g) for g in range(GROUP)]
            + [in_spec(g) for g in range(GROUP)]
            + [whole, whole],
            out_specs=pl.BlockSpec((rows, breadth), lambda s, o, c, k: (s, 0)),
            scratch_shapes=[pltpu.VMEM((rows, breadth), a_rows.dtype)],
        ),
        name="ortho",
    )(own_at, in_at, kind, *([a_rows] * GROUP), *([received] * GROUP), high, low)


def on_device(a_rows, heights, destination):
    breadth = a_rows.shape[1]
    size_gy = lax.axis_size("gy")
    devices = lax.axis_size("gx") * size_gy
    group_pos = lax.axis_index("gy")
    my_index = lax.axis_index("gx") * size_gy + group_pos
    group_base = my_index - group_pos
    stored = a_rows.shape[0] // TILE
    tile_ids = jnp.arange(stored, dtype=jnp.int32)
    peer_ids = jnp.arange(size_gy, dtype=jnp.int32)
    slot_ids = jnp.arange(SLOTS, dtype=jnp.int32)
    tile_live = tile_ids[None, :] < heights[:, None]
    target_dev = destination // SLOTS
    target_slot = destination % SLOTS
    own_live = tile_live[group_pos]
    own_dev = target_dev[group_pos]
    own_slot = target_slot[group_pos]
    leaving = own_live & (own_dev != my_index)
    chosen = leaving[None, :] & (own_dev[None, :] - group_base == peer_ids[:, None])
    send_index = jnp.sum(jnp.where(chosen, tile_ids[None, :], 0), axis=1)
    arriving = tile_live & (target_dev == my_index) & (peer_ids[:, None] != group_pos)
    arrive_slot = jnp.sum(jnp.where(arriving, target_slot, 0), axis=1)
    arrive_has = jnp.any(arriving, axis=1)
    staying = own_live & (own_dev == my_index)
    own_match = staying[None, :] & (own_slot[None, :] == slot_ids[:, None])
    in_match = arrive_has[None, :] & (arrive_slot[None, :] == slot_ids[:, None])
    own_has = jnp.any(own_match, axis=1)
    in_has = jnp.any(in_match, axis=1)
    own_at = carried(jnp.sum(jnp.where(own_match, tile_ids[None, :], 0), axis=1), own_has)
    in_at = carried(jnp.sum(jnp.where(in_match, peer_ids[None, :], 0), axis=1), in_has)
    kind = jnp.where(own_has, 1, jnp.where(in_has, 2, 0)).astype(jnp.int32)
    root_scale = math.sqrt(devices * SLOTS * TILE)
    sizes = grid_sizes()
    height = lax.dynamic_slice(heights, (group_pos,), (1,))
    packed, outgoing = local_gram(a_rows, height, send_index, STREAMS * devices)
    packed = reduce_all(packed, sizes)
    packed, outgoing = lax.optimization_barrier((packed, outgoing))
    received = lax.all_to_all(
        outgoing.reshape(-1, TILE, breadth), "gy", split_axis=0, concat_axis=0, tiled=True
    ).reshape(-1, breadth)
    factor_r, high, low = factor(packed, breadth, root_scale)
    ortho_rows = orthonormal(a_rows, received, own_at, in_at, kind, high, low, root_scale)
    return (ortho_rows, factor_r)


def solution(mesh):
    placed = (P(("gx", "gy"), None), P("gx"), P("gx", None))
    return jax.shard_map(
        on_device,
        mesh=mesh,
        in_specs=placed,
        out_specs=(P(("gx", "gy"), None), P()),
        check_vma=False,
    )
```
